32 devices in a mesh: gx: 16 (over z, x, core), gy: 2 (over y).
Axes of the slice: x: 2, y: 2, z: 4, core: 2. Of those that a mesh axis runs over, the one named last changes fastest.
Arguments:
- temp_old: float32 [256, 64, 1024], P('gx', 'gy'), may hold values from -6 to 6
- capacity: float32 [256, 64, 1024], P('gx', 'gy'), may hold values from 0.05 to 0.5
- soil_class: int32 [256, 64, 1024], P('gx', 'gy'), may hold values from 0 to 7
- cond_table: float32 [8], replicated, may hold values from 0.3 to 3
- losses: float32 [8192, 128], P(('gx', 'gy')), may hold values from 0.1 to 10
- owner: int32 [8192, 1], P(('gx', 'gy')), may hold values from 0 to 1; in each aligned block of 256 rows (0 to 255, 256 to 511, ...) at most 256 rows name the same one
- column: int32 [8192], P(('gx', 'gy')), may hold values from 0 to 511
- injection: float32 [128, 1024], replicated, may hold values from -0.5 to 0.5
Outputs:
- temp_new: float32 [256, 64, 1024], P('gx', 'gy')
The draws below stay inside these ranges and needn't reach their ends.
Inputs may be any that keep to these rules, and one draw needn't show every extreme that they name: In each device's block of 256 rows no owner is named by more than 256 rows, a bound that some block reaches.
All inputs are finite; a program needn't handle non-finite values.
Results may differ from the reference program's by a relative error of at most 0.000061.
Values sent between devices are 32-bit elements; how exact they have to be, the bound alone decides.
A program may use at most 64 MiB of HBM per device.

```python
import math
import jax
import jax.numpy as jnp
import numpy as np
from jax import lax

CX = 16
CY = 32
NZ = 1024
SWEEPS = 4
NCLS = 8
LW = 128
SEG_DEV = 256
CAP = 256
NX = 256
NY = 64
NSEG = 8192
N_GY = 2


def with_ends(values, rng, smallest, top_value):
    longest = values.shape.index(max(values.shape))
    spots = []
    for shift in (0, 1):
        where = [jax.random.randint(jax.random.fold_in(rng, axis), (), 0, length) for axis, length in enumerate(values.shape)]
        where[longest] = (where[longest] + shift) % values.shape[longest]
        spots.append(tuple(where))
    return values.at[spots[0]].set(smallest).at[spots[1]].set(top_value)


def shard_levels(rng, dims, pieces, low, largest):
    def one(axis_at, shards_of):
        draws = jax.random.uniform(jax.random.fold_in(jax.random.fold_in(rng, 6), axis_at), (shards_of,), jnp.float32, low / len(pieces), largest / len(pieces))
        return jnp.repeat(jnp.exp(draws), dims[axis_at] // shards_of).reshape((-1,) + (1,) * (len(dims) - axis_at - 1))

    loudness = one(*pieces[0])
    for cut in pieces[1:]:
        loudness = loudness * one(*cut)
    return loudness


def routed_block(own_key, own, number, rows, count, top, reach, slope):
    order = jax.random.permutation(own_key, count)
    crowded, ordinary = shares(count, rows * top, reach, slope, True), shares(count, rows * top, reach, slope, False)
    places = jnp.arange(count)

    def named(tallies, rotation):
        used = int((tallies > 0).sum())
        fixed = max(1, used // 4)
        shifted = fixed + (places - fixed + rotation * (used - fixed)) % max(1, count - fixed)
        return jnp.zeros((count,), jnp.int32).at[order[jnp.where(places < fixed, places, shifted)]].set(jnp.asarray(tallies, jnp.int32))

    tallies = jnp.where(number % 4 == 0, named(crowded, number // 4), named(ordinary, number - number // 4 - 1))
    mixed = jax.random.permutation(jax.random.fold_in(own, 3), count)
    source_of, sink = mixed[0:count // 2 * 2:2], mixed[1:count // 2 * 2:2]
    margin = jnp.minimum(tallies[source_of] - 1, reach - tallies[sink]) // 2
    margin = jnp.where((source_of == order[0]) | (sink == order[0]) | (tallies[sink] == 0), 0, jnp.maximum(margin, 0))
    shifted = jax.random.randint(jax.random.fold_in(own, 4), (count // 2,), 0, 1 << 20) % (margin + 1)
    tallies = tallies.at[source_of].add(-shifted).at[sink].add(shifted)
    labels = jnp.searchsorted(jnp.cumsum(tallies), jnp.arange(rows * top), side="right").astype(jnp.int32)
    grid = labels.reshape(top, rows).T
    grid = grid[jax.random.permutation(jax.random.fold_in(own, 1), rows)]
    rotation = jax.random.randint(jax.random.fold_in(own, 2), (rows, 1), 0, top)
    return jnp.take_along_axis(grid, (jnp.arange(top)[None, :] + rotation) % top, axis=1)


def shares(amount, total, bound, lean, full):
    portions = [(1 << 20) // math.isqrt(grade ** lean) + 1 for grade in range(1, amount + 1)]
    largest = bound if full else min(bound, max(-(-total // amount), total * portions[0] // sum(portions)))
    least = 1 if total - largest >= amount - 1 else 0
    counts, spare = [largest] + [least] * (amount - 1), total - largest - least * (amount - 1)
    while spare > 0:
        movable = [i for i in range(1, amount) if counts[i] < largest] or [i for i in range(1, amount) if counts[i] < bound]
        whole, budget = sum([portions[i] for i in movable]), spare
        for i in movable:
            addition = min(bound - counts[i], max(1, budget * portions[i] // whole), spare)
            counts[i] = counts[i] + addition
            spare = spare - addition
    return np.array(counts)


def noise(own_key, extent, deviation, most, split=(), kind=jnp.bfloat16):
    drawn = jax.random.normal(own_key, extent, jnp.float32) * deviation
    if len(split) > 0:
        drawn = shard_levels(own_key, extent, split, -0.22, 0.18) * drawn
    return jnp.clip(drawn, min=-most, max=most).astype(kind)


def setup_inputs(seed: int = 0) -> dict:
    keys = jax.random.split(jax.random.key(seed), 9)
    temp_old = noise(keys[0], (NX, NY, NZ), 1.0, 6.0, ((0, 16), (1, 2)), jnp.float32)
    capacity = jnp.clip(jnp.exp(math.log(0.5) - 2.3025851 * jax.random.uniform(keys[1], (NX, NY, NZ), jnp.float32) ** shard_levels(keys[1], (NX, NY, NZ), ((0, 16), (1, 2)), -0.2, 0.2)), 0.05, 0.5)
    soil_class = with_ends(jax.random.randint(keys[2], (NX, NY, NZ), 0, NCLS), jax.random.fold_in(keys[2], 1), 0, NCLS - 1).astype(jnp.int32)
    cond_table = jnp.clip(jnp.exp(jax.random.uniform(keys[3], (NCLS,), jnp.float32, math.log(0.3), math.log(3.0))), 0.3, 3.0)
    losses = jnp.clip(jnp.exp(math.log(10.0) - 4.6051702 * jax.random.uniform(keys[4], (NSEG, LW), jnp.float32) ** shard_levels(keys[4], (NSEG, LW), ((0, 32),), -0.2, 0.2)), 0.1, 10.0)
    owner_keys = jax.random.split(jax.random.fold_in(keys[5], 1), NSEG // SEG_DEV)
    owner_turns = jax.random.permutation(jax.random.fold_in(keys[5], 3), NSEG // SEG_DEV)
    owner = jax.vmap(lambda own, number: routed_block(jax.random.fold_in(keys[5], 2), own, number, SEG_DEV, N_GY, 1, CAP, 2))(owner_keys, owner_turns).reshape((NSEG, 1))
    column = with_ends(jax.random.randint(keys[6], (NSEG,), 0, CX * CY), jax.random.fold_in(keys[6], 1), 0, (CX * CY) - 1).astype(jnp.int32)
    injection = noise(keys[7], (LW, NZ), LW ** -0.5, 0.5, (), jnp.float32)
    return dict(temp_old=temp_old, capacity=capacity, soil_class=soil_class, cond_table=cond_table, losses=losses, owner=owner, column=column, injection=injection)


def face_terms(cond_pad):
    center = cond_pad[1:-1, 1:-1, 1:-1]
    return [0.5 * (center + cond_pad[2:, 1:-1, 1:-1]), 0.5 * (center + cond_pad[:-2, 1:-1, 1:-1]),
            0.5 * (center + cond_pad[1:-1, 2:, 1:-1]), 0.5 * (center + cond_pad[1:-1, :-2, 1:-1]),
            0.5 * (center + cond_pad[1:-1, 1:-1, 2:]), 0.5 * (center + cond_pad[1:-1, 1:-1, :-2])]


def neighbour_sum(faces, temp_pad):
    total = faces[0] * temp_pad[2:, 1:-1, 1:-1] + faces[1] * temp_pad[:-2, 1:-1, 1:-1]
    total = total + faces[2] * temp_pad[1:-1, 2:, 1:-1] + faces[3] * temp_pad[1:-1, :-2, 1:-1]
    total = total + faces[4] * temp_pad[1:-1, 1:-1, 2:] + faces[5] * temp_pad[1:-1, 1:-1, :-2]
    return total


def reference(temp_old, capacity, soil_class, cond_table, losses, owner, column, injection):
    cond = jnp.zeros(temp_old.shape, jnp.float32)
    for klass in range(NCLS):
        cond = cond + jnp.where(soil_class == klass, cond_table[klass], jnp.float32(0.0))
    faces = face_terms(jnp.pad(cond, 1))
    diag = capacity + faces[0] + faces[1] + faces[2] + faces[3] + faces[4] + faces[5]
    profile = jnp.dot(losses, injection, precision=lax.Precision.HIGHEST, preferred_element_type=jnp.float32)
    rows = jnp.arange(NSEG, dtype=jnp.int32)
    row_x = (rows // SEG_DEV // N_GY) * CX + column // CY
    row_y = owner[:, 0] * CY + column % CY
    source = jnp.zeros((NX * NY, NZ), jnp.float32).at[row_x * NY + row_y].add(profile)
    rhs = capacity * temp_old + source.reshape(NX, NY, NZ)
    temp = temp_old
    for sweep in range(SWEEPS):
        nbsum = neighbour_sum(faces, jnp.pad(temp, 1))
        temp = temp + 0.8 * (rhs - diag * temp + nbsum) / diag
    return temp
```

```python
import functools

import jax
import jax.numpy as jnp
from jax import lax
from jax.experimental import pallas as pl
from jax.experimental.pallas import tpu as pltpu
from jax.sharding import PartitionSpec as P

SWEEPS = 4
F32 = jnp.float32
BF16 = jnp.bfloat16
MESH = pl.DeviceIdType.MESH


def split(x):
    hi = x.astype(BF16)
    return hi, (x - hi.astype(F32)).astype(BF16)


def kernel(
    n_gx, n_gy, t_hbm, cap_hbm, cls_hbm, table, loss_hbm, own_hbm, col_hbm, inj_hbm, out_hbm,
    t0, t1, cap, cls, inj, loss, own, col, cond, gx, gy, gz, half_w, base, source,
    halo_x, halo_y, cls_x, cls_y, stage_y, stage_cls, edge_y, chalo_y,
    load_sem, out_sem, xsend, xrecv, ysend, yrecv, lsend, lrecv,
):
    cx, cy, nz = cap.shape
    ncls = table.shape[0]
    me_x, me_y = lax.axis_index("gx"), lax.axis_index("gy")
    has = ((me_x > 0, me_x < n_gx - 1), (me_y > 0, me_y < n_gy - 1))
    other = ((me_x - 1, me_x + 1), (me_y - 1, me_y + 1))
    bufs = (t0, t1)

    loads = [
        pltpu.make_async_copy(src, dst, load_sem.at[n])
        for n, (src, dst) in enumerate((
            (t_hbm, t0), (cls_hbm, cls), (cap_hbm, cap), (loss_hbm, loss.at[0]),
            (own_hbm, own.at[0]), (col_hbm, col.at[0]), (inj_hbm, inj),
        ))
    ]
    for copy in loads:
        copy.start()

    barrier = pltpu.get_barrier_semaphore()
    for side in range(2):
        @pl.when(has[0][side])
        def _():
            pl.semaphore_signal(barrier, inc=1, device_id=(other[0][side], me_y), device_id_type=MESH)
    partners = [lax.rem(me_y + d, n_gy) for d in range(1, n_gy)]
    for partner in partners:
        pl.semaphore_signal(barrier, inc=1, device_id=(me_x, partner), device_id_type=MESH)
    pl.semaphore_wait(barrier, n_gy - 1 + jnp.where(has[0][0], 1, 0) + jnp.where(has[0][1], 1, 0))

    def remote(src, dst, send, recv, axis, side):
        target = (other[0][side], me_y) if axis == 0 else (me_x, other[1][side])
        return pltpu.make_async_remote_copy(
            src_ref=src, dst_ref=dst, send_sem=send, recv_sem=recv, device_id=target, device_id_type=MESH
        )

    def x_copy(k, side, src):
        dst = cls_x.at[1 - side] if k == SWEEPS else halo_x.at[k, 1 - side]
        return remote(src, dst, xsend.at[k, side], xrecv.at[k, 1 - side], 0, side)

    def y_copy(k, side):
        src, dst = (stage_cls.at[side], cls_y.at[1 - side]) if k == SWEEPS else (stage_y.at[k, side], halo_y.at[k, 1 - side])
        return remote(src, dst, ysend.at[k, side], yrecv.at[k, 1 - side], 1, side)

    def x_plane(k, side):
        plane = (0, cx - 1)[side]
        if k == SWEEPS:
            return cls_hbm.at[plane]
        return t_hbm.at[plane] if k == 0 else bufs[k % 2].at[plane]

    def send_x(k):
        for side in range(2):
            @pl.when(has[0][side])
            def _():
                x_copy(k, side, x_plane(k, side)).start()

    def send_y(k):
        for side in range(2):
            @pl.when(has[1][side])
            def _():
                y_copy(k, side).start()

    def await_x(k):
        for side in range(2):
            @pl.when(has[0][side])
            def _():
                x_copy(k, 1 - side, x_plane(k, 1 - side)).wait_recv()

    def await_y(k):
        for side in range(2):
            @pl.when(has[1][side])
            def _():
                y_copy(k, 1 - side).wait_recv()

    def sent_x(k):
        for side in range(2):
            @pl.when(has[0][side])
            def _():
                x_copy(k, side, x_plane(k, side)).wait_send()

    def sent_y(k):
        for side in range(2):
            @pl.when(has[1][side])
            def _():
                y_copy(k, side).wait_send()

    send_x(SWEEPS)
    send_x(0)
    loss_copies = [
        pltpu.make_async_remote_copy(
            src_ref=src, dst_ref=dst.at[d], send_sem=lsend.at[n, d], recv_sem=lrecv.at[n, d],
            device_id=(me_x, partners[d - 1]), device_id_type=MESH,
        )
        for d in range(1, n_gy)
        for n, (src, dst) in enumerate(((loss_hbm, loss), (own_hbm, own), (col_hbm, col)))
    ]
    for copy in loss_copies:
        copy.start()

    for axis, halos, ids in ((0, halo_x, cls_x), (1, halo_y, cls_y)):
        for side in range(2):
            @pl.when(jnp.logical_not(has[axis][side]))
            def _():
                ids[side] = jnp.zeros(ids.shape[1:], jnp.int32)
                for k in range(SWEEPS):
                    halos[k, side] = jnp.zeros(halos.shape[2:], F32)

    loads[1].wait()
    for side in range(2):
        stage_cls[side] = cls[:, (0, cy - 1)[side], :]
    send_y(SWEEPS)
    loads[0].wait()
    for side in range(2):
        stage_y[0, side] = t0[:, (0, cy - 1)[side], :]
    send_y(0)

    def look_up(ids):
        values = jnp.full(ids.shape, table[0], F32)
        for klass in range(1, ncls):
            values = jnp.where(ids == klass, table[klass], values)
        return values

    @pl.loop(0, cx)
    def _(i):
        cond[i + 1] = look_up(cls[i])

    for copy in loads[2:]:
        copy.wait()
    inj_hi, inj_lo = split(inj[...])
    inj_hi = jnp.concatenate([inj_hi, inj_hi], axis=0)
    inj_lo = jnp.concatenate([inj_lo, inj_lo], axis=0)
    for copy in loss_copies:
        copy.wait_recv()
    lw = loss.shape[2]
    spread = None
    for d in range(n_gy):
        hit = jnp.where(own[d] == me_y, col[d], -1)
        picker = hit == lax.broadcasted_iota(jnp.int32, (cx * cy, hit.shape[1]), 0)
        picker = jnp.where(picker, F32(1.0), F32(0.0)).astype(BF16)
        part = jnp.dot(picker, jnp.concatenate(split(loss[d]), axis=1), preferred_element_type=F32)
        spread = part if spread is None else spread + part
    spread = jnp.concatenate(split(spread[:, :lw] + spread[:, lw:]), axis=1)
    source[...] = jnp.dot(spread, inj_hi, preferred_element_type=F32) + jnp.dot(spread, inj_lo, preferred_element_type=F32)

    await_x(SWEEPS)
    for side in range(2):
        cond[(0, cx + 1)[side]] = look_up(cls_x[side]) * jnp.where(has[0][side], F32(1.0), F32(0.0))
    await_y(SWEEPS)
    for side in range(2):
        chalo_y[side] = look_up(cls_y[side]) * jnp.where(has[1][side], F32(1.0), F32(0.0))

    gx[cx] = cond[cx] + cond[cx + 1]

    @pl.loop(0, cx)
    def _(i):
        row = lax.broadcasted_iota(jnp.int32, (cy, nz), 0)
        lane = lax.broadcasted_iota(jnp.int32, (cy, nz), 1)
        low, here, high = cond[i], cond[i + 1], cond[i + 2]
        gx[i] = low + here
        y_low, y_high = chalo_y[0, pl.ds(i, 1), :], chalo_y[1, pl.ds(i, 1), :]
        after = pltpu.roll(here, cy - 1, 0)
        gy[i] = jnp.where(row == cy - 1, F32(0.0), here + after)
        total = low + high + jnp.where(row == cy - 1, y_high, after)
        total = total + jnp.where(row == 0, y_low, pltpu.roll(here, 1, 0))
        after = jnp.where(lane == nz - 1, F32(0.0), pltpu.roll(here, nz - 1, 1))
        gz[i] = jnp.where(lane == nz - 1, F32(0.0), here + after)
        total = total + after + jnp.where(lane == 0, F32(0.0), pltpu.roll(here, 1, 1))
        weight = 0.4 / (cap[i] + (3.0 * here + 0.5 * total))
        half_w[i] = weight
        base[i] = 2.0 * weight * (cap[i] * t0[i] + source[pl.ds(pl.multiple_of(i * cy, cy), cy), :])
        edge_y[0, pl.ds(i, 1), :] = weight[:1] * (here[:1] + y_low)
        edge_y[1, pl.ds(i, 1), :] = weight[cy - 1:] * (here[cy - 1:] + y_high)

    def advance(now, new, i, low, high):
        here = now[i]
        total = gx[i] * low + gx[i + 1] * high
        face = gy[i]
        total = total + face * pltpu.roll(here, cy - 1, 0) + pltpu.roll(face * here, 1, 0)
        face = gz[i]
        total = total + face * pltpu.roll(here, nz - 1, 1) + pltpu.roll(face * here, 1, 1)
        new[i] = 0.2 * here + base[i] + half_w[i] * total

    for k in range(SWEEPS):
        now, new = bufs[k % 2], bufs[(k + 1) % 2]

        @pl.loop(1, cx - 1)
        def _(i):
            advance(now, new, i, now[i - 1], now[i + 1])

        if k >= 2:
            sent_x(k - 1)
        await_x(k)
        advance(now, new, 0, halo_x[k, 0], now[1])
        advance(now, new, cx - 1, now[cx - 2], halo_x[k, 1])
        await_y(k)
        for side in range(2):
            spot = (0, cy - 1)[side]
            fixed = new[:, spot, :] + edge_y[side] * halo_y[k, side]
            new[:, spot, :] = fixed
            if k + 1 < SWEEPS:
                stage_y[k + 1, side] = fixed
        if k + 1 < SWEEPS:
            send_x(k + 1)
            send_y(k + 1)

    done = pltpu.make_async_copy(bufs[SWEEPS % 2], out_hbm, out_sem)
    done.start()
    sent_x(SWEEPS)
    sent_x(0)
    sent_x(SWEEPS - 1)
    for k in range(SWEEPS + 1):
        sent_y(k)
    for copy in loss_copies:
        copy.wait_send()
    done.wait()


def solution(mesh):
    n_gx, n_gy = mesh.shape["gx"], mesh.shape["gy"]

    def shards(temp_old, capacity, soil_class, cond_table, losses, owner, column, injection):
        cx, cy, nz = temp_old.shape
        segments, lw = losses.shape
        owner, column = owner.reshape(1, segments), column.reshape(1, segments)
        field = pltpu.VMEM((cx, cy, nz), F32)
        any_spec = pl.BlockSpec(memory_space=pl.ANY)
        dma = pltpu.SemaphoreType.DMA
        return pl.pallas_call(
            functools.partial(kernel, n_gx, n_gy),
            out_shape=jax.ShapeDtypeStruct(temp_old.shape, F32),
            in_specs=[any_spec] * 3 + [pl.BlockSpec(memory_space=pltpu.SMEM)] + [any_spec] * 4,
            out_specs=any_spec,
            scratch_shapes=[
                field, field, field,
                pltpu.VMEM((cx, cy, nz), jnp.int32),
                pltpu.VMEM(injection.shape, F32),
                pltpu.VMEM((n_gy, segments, lw), F32),
                pltpu.VMEM((n_gy, 1, segments), jnp.int32),
                pltpu.VMEM((n_gy, 1, segments), jnp.int32),
                pltpu.VMEM((cx + 2, cy, nz), F32),
                pltpu.VMEM((cx + 1, cy, nz), F32),
                field, field, field, field,
                pltpu.VMEM((cx * cy, nz), F32),
                pltpu.VMEM((SWEEPS, 2, cy, nz), F32),
                pltpu.VMEM((SWEEPS, 2, cx, nz), F32),
                pltpu.VMEM((2, cy, nz), jnp.int32),
                pltpu.VMEM((2, cx, nz), jnp.int32),
                pltpu.VMEM((SWEEPS, 2, cx, nz), F32),
                pltpu.VMEM((2, cx, nz), jnp.int32),
                pltpu.VMEM((2, cx, nz), F32),
                pltpu.VMEM((2, cx, nz), F32),
                dma((7,)), dma(()),
                dma((SWEEPS + 1, 2)), dma((SWEEPS + 1, 2)), dma((SWEEPS + 1, 2)), dma((SWEEPS + 1, 2)),
                dma((3, n_gy)), dma((3, n_gy)),
            ],
            compiler_params=pltpu.CompilerParams(
                collective_id=0, has_side_effects=True, vmem_limit_bytes=60 * 2**20
            ),
        )(temp_old, capacity, soil_class, cond_table, losses, owner, column, injection)

    return jax.shard_map(
        shards,
        mesh=mesh,
        in_specs=(
            P("gx", "gy", None),
            P("gx", "gy", None),
            P("gx", "gy", None),
            P(),
            P(("gx", "gy"), None),
            P(("gx", "gy"), None),
            P(("gx", "gy")),
            P(),
        ),
        out_specs=P("gx", "gy", None),
        check_vma=False,
    )
```

```python
import functools

import jax
import jax.numpy as jnp
from jax import lax
from jax.experimental import pallas as pl
from jax.experimental.pallas import tpu as pltpu
from jax.sharding import PartitionSpec as P

SWEEPS = 4
VMEM_LIMIT = 64_946_176
F32 = jnp.float32
BF16 = jnp.bfloat16
MESH = pl.DeviceIdType.MESH


def split(x):
    hi = x.astype(BF16)
    return hi, (x - hi.astype(F32)).astype(BF16)


def kernel(
    n_gx, n_gy, t_hbm, cap_hbm, cls_hbm, table, loss_hbm, own_hbm, col_hbm, inj_hbm, out,
    t0, t1, cap, cls, inj, loss, own, col, cond, gx, gy, gz, half_w, base, source,
    halo_x, halo_y, cls_x, cls_y, stage_y, stage_cls, edge_y, chalo_y,
    load_sem, xsend, xrecv, ysend, yrecv, lsend, lrecv,
):
    cx, cy, nz = cap.shape
    ncls = table.shape[0]
    me_x, me_y = lax.axis_index("gx"), lax.axis_index("gy")
    has = ((me_x > 0, me_x < n_gx - 1), (me_y > 0, me_y < n_gy - 1))
    other = ((me_x - 1, me_x + 1), (me_y - 1, me_y + 1))
    bufs = [(t0, t1)[k % 2] for k in range(SWEEPS)] + [out]

    loads = [
        pltpu.make_async_copy(src, dst, load_sem.at[n])
        for n, (src, dst) in enumerate((
            (t_hbm, t0), (cls_hbm, cls), (cap_hbm, cap), (loss_hbm, loss.at[0]),
            (own_hbm, own.at[0]), (col_hbm, col.at[0]), (inj_hbm, inj),
        ))
    ]
    for copy in loads:
        copy.start()

    barrier = pltpu.get_barrier_semaphore()
    for side in range(2):
        @pl.when(has[0][side])
        def _():
            pl.semaphore_signal(barrier, inc=1, device_id=(other[0][side], me_y), device_id_type=MESH)
    partners = [lax.rem(me_y + d, n_gy) for d in range(1, n_gy)]
    for partner in partners:
        pl.semaphore_signal(barrier, inc=1, device_id=(me_x, partner), device_id_type=MESH)
    pl.semaphore_wait(barrier, n_gy - 1 + jnp.where(has[0][0], 1, 0) + jnp.where(has[0][1], 1, 0))

    def remote(src, dst, send, recv, axis, side):
        target = (other[0][side], me_y) if axis == 0 else (me_x, other[1][side])
        return pltpu.make_async_remote_copy(
            src_ref=src, dst_ref=dst, send_sem=send, recv_sem=recv, device_id=target, device_id_type=MESH
        )

    def x_copy(k, side, src):
        dst = cls_x.at[1 - side] if k == SWEEPS else halo_x.at[k, 1 - side]
        return remote(src, dst, xsend.at[k, side], xrecv.at[k, 1 - side], 0, side)

    def y_copy(k, side):
        src, dst = (stage_cls.at[side], cls_y.at[1 - side]) if k == SWEEPS else (stage_y.at[k, side], halo_y.at[k, 1 - side])
        return remote(src, dst, ysend.at[k, side], yrecv.at[k, 1 - side], 1, side)

    def x_plane(k, side):
        plane = (0, cx - 1)[side]
        if k == SWEEPS:
            return cls_hbm.at[plane]
        return t_hbm.at[plane] if k == 0 else bufs[k].at[plane]

    def send_x(k):
        for side in range(2):
            @pl.when(has[0][side])
            def _():
                x_copy(k, side, x_plane(k, side)).start()

    def send_y(k):
        for side in range(2):
            @pl.when(has[1][side])
            def _():
                y_copy(k, side).start()

    def await_x(k):
        for side in range(2):
            @pl.when(has[0][side])
            def _():
                x_copy(k, 1 - side, x_plane(k, 1 - side)).wait_recv()

    def await_y(k):
        for side in range(2):
            @pl.when(has[1][side])
            def _():
                y_copy(k, 1 - side).wait_recv()

    def sent_x(k):
        for side in range(2):
            @pl.when(has[0][side])
            def _():
                x_copy(k, side, x_plane(k, side)).wait_send()

    def sent_y(k):
        for side in range(2):
            @pl.when(has[1][side])
            def _():
                y_copy(k, side).wait_send()

    send_x(SWEEPS)
    send_x(0)
    loss_copies = [
        pltpu.make_async_remote_copy(
            src_ref=src, dst_ref=dst.at[d], send_sem=lsend.at[n, d], recv_sem=lrecv.at[n, d],
            device_id=(me_x, partners[d - 1]), device_id_type=MESH,
        )
        for d in range(1, n_gy)
        for n, (src, dst) in enumerate(((loss_hbm, loss), (own_hbm, own), (col_hbm, col)))
    ]

    loads[1].wait()
    for side in range(2):
        stage_cls[side] = cls[:, (0, cy - 1)[side], :]
    send_y(SWEEPS)
    for copy in loss_copies:
        copy.start()
    loads[0].wait()
    for side in range(2):
        stage_y[0, side] = t0[:, (0, cy - 1)[side], :]
    send_y(0)

    for axis, halos, ids in ((0, halo_x, cls_x), (1, halo_y, cls_y)):
        for side in range(2):
            @pl.when(jnp.logical_not(has[axis][side]))
            def _():
                ids[side] = jnp.zeros(ids.shape[1:], jnp.int32)
                for k in range(SWEEPS):
                    halos[k, side] = jnp.zeros(halos.shape[2:], F32)

    def look_up(ids):
        values = jnp.full(ids.shape, table[0], F32)
        for klass in range(1, ncls):
            values = jnp.where(ids == klass, table[klass], values)
        return values

    @pl.loop(0, cx)
    def _(i):
        cond[i + 1] = look_up(cls[i])

    await_y(SWEEPS)
    for side in range(2):
        chalo_y[side] = look_up(cls_y[side]) * jnp.where(has[1][side], F32(1.0), F32(0.0))
    loads[2].wait()

    def prepare(i):
        row = lax.broadcasted_iota(jnp.int32, (cy, nz), 0)
        lane = lax.broadcasted_iota(jnp.int32, (cy, nz), 1)
        low, here, high = cond[i], cond[i + 1], cond[i + 2]
        gx[i] = low + here
        y_low, y_high = chalo_y[0, pl.ds(i, 1), :], chalo_y[1, pl.ds(i, 1), :]
        after = pltpu.roll(here, cy - 1, 0)
        gy[i] = jnp.where(row == cy - 1, F32(0.0), here + after)
        total = low + high + jnp.where(row == cy - 1, y_high, after)
        total = total + jnp.where(row == 0, y_low, pltpu.roll(here, 1, 0))
        after = jnp.where(lane == nz - 1, F32(0.0), pltpu.roll(here, nz - 1, 1))
        gz[i] = jnp.where(lane == nz - 1, F32(0.0), here + after)
        total = total + after + jnp.where(lane == 0, F32(0.0), pltpu.roll(here, 1, 1))
        weight = 0.4 / (cap[i] + (3.0 * here + 0.5 * total))
        half_w[i] = weight
        edge_y[0, pl.ds(i, 1), :] = weight[:1] * (here[:1] + y_low)
        edge_y[1, pl.ds(i, 1), :] = weight[cy - 1:] * (here[cy - 1:] + y_high)

    @pl.loop(1, cx - 1)
    def _(i):
        prepare(i)

    for copy in loads[3:]:
        copy.wait()
    inj_hi, inj_lo = split(inj[...])
    inj_hi = jnp.concatenate([inj_hi, inj_hi], axis=0)
    inj_lo = jnp.concatenate([inj_lo, inj_lo], axis=0)
    for copy in loss_copies:
        copy.wait_recv()
    lw = loss.shape[2]
    spread = None
    for d in range(n_gy):
        hit = jnp.where(own[d] == me_y, col[d], -1)
        picker = hit == lax.broadcasted_iota(jnp.int32, (cx * cy, hit.shape[1]), 0)
        picker = jnp.where(picker, F32(1.0), F32(0.0)).astype(BF16)
        part = jnp.dot(picker, jnp.concatenate(split(loss[d]), axis=1), preferred_element_type=F32)
        spread = part if spread is None else spread + part
    spread = jnp.concatenate(split(spread[:, :lw] + spread[:, lw:]), axis=1)
    source[...] = jnp.dot(spread, inj_hi, preferred_element_type=F32) + jnp.dot(spread, inj_lo, preferred_element_type=F32)

    await_x(SWEEPS)
    for side in range(2):
        cond[(0, cx + 1)[side]] = look_up(cls_x[side]) * jnp.where(has[0][side], F32(1.0), F32(0.0))
    prepare(0)
    prepare(cx - 1)
    gx[cx] = cond[cx] + cond[cx + 1]

    def advance(k, i, low, high):
        here = bufs[k][i]
        weight = half_w[i]
        total = gx[i] * low + gx[i + 1] * high
        face = gy[i]
        total = total + face * pltpu.roll(here, cy - 1, 0) + pltpu.roll(face * here, 1, 0)
        face = gz[i]
        total = total + face * pltpu.roll(here, nz - 1, 1) + pltpu.roll(face * here, 1, 1)
        if k == 0:
            start = i * cy if isinstance(i, int) else pl.multiple_of(i * cy, cy)
            known = 2.0 * weight * (cap[i] * here + source[pl.ds(start, cy), :])
            base[i] = known
        else:
            known = base[i]
        bufs[k + 1][i] = 0.2 * here + known + weight * total

    def fix_plane(k, i):
        new = bufs[k + 1]
        for side in range(2):
            spot = (0, cy - 1)[side]
            fixed = new[i, spot:spot + 1, :] + edge_y[side, pl.ds(i, 1), :] * halo_y[k, side, pl.ds(i, 1), :]
            new[i, spot:spot + 1, :] = fixed
            stage_y[k + 1, side, pl.ds(i, 1), :] = fixed

    def fix_all(k):
        new = bufs[k + 1]
        for side in range(2):
            spot = (0, cy - 1)[side]
            fixed = new[:, spot, :] + edge_y[side] * halo_y[k, side]
            new[:, spot, :] = fixed
            if k + 1 < SWEEPS:
                stage_y[k + 1, side] = fixed

    def edges(k):
        await_x(k)
        advance(k, 0, halo_x[k, 0], bufs[k][1])
        advance(k, cx - 1, bufs[k][cx - 2], halo_x[k, 1])
        await_y(k)

    def middle(k, fix):
        @pl.loop(1, cx - 1)
        def _(i):
            advance(k, i, bufs[k][i - 1], bufs[k][i + 1])
            if fix:
                fix_plane(k, i)

    edges(0)
    fix_plane(0, 0)
    fix_plane(0, cx - 1)
    send_x(1)
    middle(0, True)
    send_y(1)
    for k in range(1, SWEEPS):
        middle(k, False)
        if 2 <= k < SWEEPS - 1:
            sent_x(k - 1)
        edges(k)
        fix_all(k)
        if k + 1 < SWEEPS:
            send_x(k + 1)
            send_y(k + 1)

    sent_x(SWEEPS)
    sent_x(0)
    for k in range(max(1, SWEEPS - 2), SWEEPS):
        sent_x(k)
    for k in range(SWEEPS + 1):
        sent_y(k)
    for copy in loss_copies:
        copy.wait_send()


def solution(mesh):
    n_gx, n_gy = mesh.shape["gx"], mesh.shape["gy"]

    def shards(temp_old, capacity, soil_class, cond_table, losses, owner, column, injection):
        cx, cy, nz = temp_old.shape
        segments, lw = losses.shape
        owner, column = owner.reshape(1, segments), column.reshape(1, segments)
        field = pltpu.VMEM((cx, cy, nz), F32)
        any_spec = pl.BlockSpec(memory_space=pltpu.HBM)
        dma = pltpu.SemaphoreType.DMA
        return pl.pallas_call(
            functools.partial(kernel, n_gx, n_gy),
            out_shape=pltpu.VMEM(temp_old.shape, F32),
            in_specs=[any_spec] * 3 + [pl.BlockSpec(memory_space=pltpu.SMEM)] + [any_spec] * 4,
            out_specs=pl.BlockSpec(memory_space=pltpu.VMEM),
            scratch_shapes=[
                field, field, field,
                pltpu.VMEM((cx, cy, nz), jnp.int32),
                pltpu.VMEM(injection.shape, F32),
                pltpu.VMEM((n_gy, segments, lw), F32),
                pltpu.VMEM((n_gy, 1, segments), jnp.int32),
                pltpu.VMEM((n_gy, 1, segments), jnp.int32),
                pltpu.VMEM((cx + 2, cy, nz), F32),
                pltpu.VMEM((cx + 1, cy, nz), F32),
                field, field, field, field,
                pltpu.VMEM((cx * cy, nz), F32),
                pltpu.VMEM((SWEEPS, 2, cy, nz), F32),
                pltpu.VMEM((SWEEPS, 2, cx, nz), F32),
                pltpu.VMEM((2, cy, nz), jnp.int32),
                pltpu.VMEM((2, cx, nz), jnp.int32),
                pltpu.VMEM((SWEEPS, 2, cx, nz), F32),
                pltpu.VMEM((2, cx, nz), jnp.int32),
                pltpu.VMEM((2, cx, nz), F32),
                pltpu.VMEM((2, cx, nz), F32),
                dma((7,)),
                dma((SWEEPS + 1, 2)), dma((SWEEPS + 1, 2)), dma((SWEEPS + 1, 2)), dma((SWEEPS + 1, 2)),
                dma((3, n_gy)), dma((3, n_gy)),
            ],
            compiler_params=pltpu.CompilerParams(
                collective_id=0, has_side_effects=True, vmem_limit_bytes=VMEM_LIMIT
            ),
        )(temp_old, capacity, soil_class, cond_table, losses, owner, column, injection)

    return jax.shard_map(
        shards,
        mesh=mesh,
        in_specs=(
            P("gx", "gy", None),
            P("gx", "gy", None),
            P("gx", "gy", None),
            P(),
            P(("gx", "gy"), None),
            P(("gx", "gy"), None),
            P(("gx", "gy")),
            P(),
        ),
        out_specs=P("gx", "gy", None),
        check_vma=False,
    )
```
